32 devices in a mesh: ta: 2 (over x), gz: 4 (over y, core), gy: 4 (over z).
Axes of the slice: x: 2, y: 2, z: 4, core: 2. Of those that a mesh axis runs over, the one named last changes fastest.
Arguments:
- near_null: float32 [8, 16, 16, 12, 12, 128], P('ta', 'gz', 'gy'), may hold values from -400 to 400
- offsets: int32 [4], replicated, may hold values from 1 to 3
- owner_slot: int32 [2, 4, 4, 16], P('ta', 'gz', 'gy'), may hold values from 0 to 15, each once within a row
Outputs:
- result: float32 [512, 2, 12, 6, 2, 256], P(('ta', 'gz', 'gy'))
The draws below stay inside these ranges and needn't reach their ends.
Inputs may be any that keep to these rules, and one draw needn't show every extreme that they name: The same offsets hold for every device. `owner_slot`: each device's row is a permutation of 0 to 15.
All inputs are finite; a program needn't handle non-finite values.
Results may differ from the reference program's by a relative error of at most 0.0001.
Values sent between devices are 32-bit elements; how exact they have to be, the bound alone decides.
A program may use at most 256 MiB of HBM per device.

```python
import jax
import jax.numpy as jnp
from jax import lax

V = 12
C = 12
AGG = 4
NX = 64
NT = 8
NZ = 16
NY = 16
NAGG = 16
N_TA = 2
N_GZ = 4
N_GY = 4


def draw_near_null(key, part):
    key_base, key_site, key_vector = jax.random.split(key, 3)
    shape = (NT, NZ, NY, V, C, 2 * NX)
    site_scale = jnp.exp(jax.random.uniform(key_site, (NT, NZ, NY, 1, 1, 2 * NX), jnp.float32) * jnp.log(10.0))
    vector_scale = jnp.exp(jax.random.uniform(key_vector, (1, 1, 1, V, 1, 1), jnp.float32) * jnp.log(10.0))
    base = jnp.clip(jax.random.normal(key_base, shape, jnp.float32), -4.0, 4.0)
    return (base * site_scale * vector_scale).astype(jnp.float32)


def with_ends(entries, rng, smallest, high):
    longest = entries.shape.index(max(entries.shape))
    spots = []
    for shift in (0, 1):
        where = [jax.random.randint(jax.random.fold_in(rng, axis), (), 0, length) for axis, length in enumerate(entries.shape)]
        where[longest] = (where[longest] + shift) % entries.shape[longest]
        spots.append(tuple(where))
    return entries.at[spots[0]].set(smallest).at[spots[1]].set(high)


def setup_inputs(seed: int = 0) -> dict:
    key_of = jax.random.split(jax.random.key(seed), 4)
    near_null = draw_near_null(jax.random.fold_in(key_of[3], 71), 0)
    offsets = with_ends(jax.random.randint(key_of[1], (4,), 1, AGG), jax.random.fold_in(key_of[1], 1), 1, AGG - 1).astype(jnp.int32)
    owner_slot = jax.vmap(lambda own: jax.random.permutation(own, NAGG))(jax.random.split(key_of[2], N_TA * N_GZ * N_GY)).reshape((N_TA, N_GZ, N_GY, NAGG)).astype(jnp.int32)
    return {"near_null": near_null, "offsets": offsets, "owner_slot": owner_slot}


ridge_scale = 0.05
top_precision = lax.Precision.HIGHEST

def factor_pass(blocks):
    norm_count = blocks.shape[3] * blocks.shape[5]
    products = jnp.einsum('nkvcas,nkwcbs->nkavbw', blocks, blocks, precision=top_precision) / norm_count
    gram_real = products[:, :, 0, :, 0, :] + products[:, :, 1, :, 1, :]
    gram_imag = products[:, :, 0, :, 1, :] - products[:, :, 1, :, 0, :]
    width = gram_real.shape[-1]
    diag_mean = lax.optimization_barrier(jnp.mean(jnp.diagonal(gram_real, axis1=2, axis2=3), axis=-1))
    ridge_term = ridge_scale * (diag_mean + 1e-06)
    gram_real = jnp.moveaxis(gram_real, (2, 3), (0, 1))
    gram_imag = jnp.moveaxis(gram_imag, (2, 3), (0, 1))
    zero_batch = jnp.zeros_like(ridge_term)
    low_real = [[zero_batch] * width for row_idx in range(width)]
    low_imag = [[zero_batch] * width for row_idx in range(width)]
    for col_idx in range(width):
        remain = gram_real[col_idx, col_idx] + ridge_term
        for mid_idx in range(col_idx):
            remain = remain - low_real[col_idx][mid_idx] * low_real[col_idx][mid_idx]
            remain = remain - low_imag[col_idx][mid_idx] * low_imag[col_idx][mid_idx]
        diag_val = jnp.sqrt(remain)
        low_real[col_idx][col_idx] = diag_val
        for row_idx in range(col_idx + 1, width):
            sum_real = gram_real[row_idx, col_idx]
            sum_imag = gram_imag[row_idx, col_idx]
            for mid_idx in range(col_idx):
                left_real = low_real[row_idx][mid_idx]
                left_imag = low_imag[row_idx][mid_idx]
                right_real = low_real[col_idx][mid_idx]
                right_imag = low_imag[col_idx][mid_idx]
                sum_real = sum_real - (left_real * right_real + left_imag * right_imag)
                sum_imag = sum_imag - (left_imag * right_real - left_real * right_imag)
            low_real[row_idx][col_idx] = sum_real / diag_val
            low_imag[row_idx][col_idx] = sum_imag / diag_val
    inv_real = [[zero_batch] * width for row_idx in range(width)]
    inv_imag = [[zero_batch] * width for row_idx in range(width)]
    for col_idx in range(width):
        inv_real[col_idx][col_idx] = 1.0 / low_real[col_idx][col_idx]
        for row_idx in range(col_idx + 1, width):
            sum_real = zero_batch
            sum_imag = zero_batch
            for mid_idx in range(col_idx, row_idx):
                left_real = low_real[row_idx][mid_idx]
                left_imag = low_imag[row_idx][mid_idx]
                right_real = inv_real[mid_idx][col_idx]
                right_imag = inv_imag[mid_idx][col_idx]
                sum_real = sum_real + left_real * right_real - left_imag * right_imag
                sum_imag = sum_imag + left_real * right_imag + left_imag * right_real
            inv_real[row_idx][col_idx] = -sum_real / low_real[row_idx][row_idx]
            inv_imag[row_idx][col_idx] = -sum_imag / low_real[row_idx][row_idx]
    map_real = jnp.stack([jnp.stack([inv_real[w_idx][v_idx] for w_idx in range(width)], axis=-1) for v_idx in range(width)], axis=-2)
    map_imag = -jnp.stack([jnp.stack([inv_imag[w_idx][v_idx] for w_idx in range(width)], axis=-1) for v_idx in range(width)], axis=-2)
    mixing = jnp.stack([jnp.stack([map_real, map_imag], axis=3), jnp.stack([-map_imag, map_real], axis=3)], axis=2)
    return jnp.einsum('nkvcas,nkavbw->nkwcbs', blocks, mixing, precision=top_precision)

def two_passes(blocks):
    return factor_pass(factor_pass(blocks))

def reference(near_null, offsets, owner_slot):
    lattice = near_null.reshape(NT, NZ, NY, V, C, 2, NX)
    lattice = jnp.roll(lattice, -offsets[0], axis=0)
    lattice = jnp.roll(lattice, -offsets[1], axis=1)
    lattice = jnp.roll(lattice, -offsets[2], axis=2)
    lattice = jnp.roll(lattice, -offsets[3], axis=6)
    half_c = C // 2
    pieces = lattice.reshape(N_TA, AGG, N_GZ, AGG, N_GY, AGG, V, 2, half_c, 2, NAGG, AGG)
    pieces = pieces.transpose(0, 2, 4, 10, 7, 6, 8, 9, 1, 3, 5, 11)
    site_count = AGG * AGG * AGG * AGG
    device_count = N_TA * N_GZ * N_GY
    flattened = pieces.reshape(device_count * NAGG, 2, V, half_c, 2, site_count)
    source_of = jnp.argsort(owner_slot, axis=-1).astype(jnp.int32)
    device_base = (jnp.arange(device_count, dtype=jnp.int32) * NAGG).reshape(N_TA, N_GZ, N_GY, 1)
    packed = jnp.take(flattened, (device_base + source_of).reshape(-1), axis=0)
    per_peer = NAGG // N_TA
    packed = packed.reshape(N_TA, N_GZ, N_GY, N_TA, per_peer, 2, V, half_c, 2, site_count)
    owned_aggs = packed.transpose(3, 1, 2, 0, 4, 5, 6, 7, 8, 9).reshape(device_count, NAGG, 2, V, half_c, 2, site_count)
    result = lax.map(two_passes, owned_aggs)
    return result.reshape(device_count * NAGG, 2, V, half_c, 2, site_count)
```

```python
import functools

import jax
import jax.numpy as jnp
from jax import lax
from jax.experimental import pallas as pl
from jax.experimental.pallas import tpu as pltpu
from jax.sharding import PartitionSpec as P

MAX_OFFSET = 3
LANES = 128


def compact_kernel(shift_ref, in_ref, out_ref):
    _, _, edge, vectors, comps, lanes = in_ref.shape
    half = lanes // 2
    shift = shift_ref[0]
    lane = lax.broadcasted_iota(jnp.int32, (comps, lanes), 1) % half
    inside = lane < half - shift
    for y in range(edge):
        for v in range(vectors):
            rows = in_ref[0, 0, y, v]
            near = pltpu.roll(rows, lanes - shift, 1)
            wrap = pltpu.roll(rows, half - shift, 1)
            out_ref[0, y, v * comps : (v + 1) * comps, :] = jnp.where(inside, near, wrap)


def compact(near_null, x_offset, t):
    _, nz, ny, vectors, comps, lanes = near_null.shape
    size = nz * ny * vectors * comps * lanes
    return pl.pallas_call(
        compact_kernel,
        grid_spec=pltpu.PrefetchScalarGridSpec(
            num_scalar_prefetch=1,
            grid=(nz,),
            in_specs=[
                pl.BlockSpec(
                    (1, 1, ny, vectors, comps, lanes), lambda z, s: (t, z, 0, 0, 0, 0)
                )
            ],
            out_specs=pl.BlockSpec((1, ny, vectors * comps, lanes), lambda z, s: (z, 0, 0, 0)),
        ),
        out_shape=jax.ShapeDtypeStruct((nz, ny, vectors * comps, lanes), jnp.float32),
        cost_estimate=pl.CostEstimate(flops=size * 4, bytes_accessed=size * 9, transcendentals=0),
    )(x_offset, near_null)


def regroup_kernel(oz, oy, edge, place_ref, own_ref, z_ref, y_ref, keep_ref, send_ref, stage):
    rows = own_ref.shape[2]
    lanes = own_ref.shape[3]
    count = edge * edge
    half = count // 2
    lane = lax.broadcasted_iota(jnp.int32, (8, lanes), 1)
    places = [place_ref[j] for j in range(count)]
    for r in range(0, rows, 8):
        units = []
        for z in range(edge):
            for y in range(edge):
                if y + oy >= edge:
                    ref, zi, yi = y_ref, z, y + oy - edge
                elif z + oz >= edge:
                    ref, zi, yi = z_ref, z + oz - edge, y + oy
                else:
                    ref, zi, yi = own_ref, z + oz, y + oy
                units.append(ref[zi, yi, r : r + 8, :])
        bit = 1
        while bit < count:
            step = bit * edge
            high = (lane & step) != 0
            fresh = list(units)
            for u in range(count):
                if not u & bit:
                    low_unit, high_unit = units[u], units[u + bit]
                    fresh[u] = jnp.where(high, pltpu.roll(high_unit, step, 1), low_unit)
                    fresh[u + bit] = jnp.where(
                        high, high_unit, pltpu.roll(low_unit, lanes - step, 1)
                    )
            units = fresh
            bit *= 2
        for j in range(count):
            stage[places[j], r : r + 8, :] = units[j]
    keep_ref[...] = stage[:half]
    send_ref[...] = stage[half:]


def regroup(oz, oy, place, own, from_z, from_y):
    edge = own.shape[0]
    rows, lanes = own.shape[2:]
    chunk = 24
    count = edge * edge
    half = count // 2
    size = count * rows * lanes
    out = jax.ShapeDtypeStruct((half, rows, lanes), jnp.float32)
    out_spec = pl.BlockSpec((half, chunk, lanes), lambda r, s: (0, r, 0))
    return pl.pallas_call(
        functools.partial(regroup_kernel, oz, oy, edge),
        grid_spec=pltpu.PrefetchScalarGridSpec(
            num_scalar_prefetch=1,
            grid=(rows // chunk,),
            in_specs=[
                pl.BlockSpec(array.shape[:2] + (chunk, lanes), lambda r, s: (0, 0, r, 0))
                for array in (own, from_z, from_y)
            ],
            out_specs=[out_spec, out_spec],
            scratch_shapes=[pltpu.VMEM((count, chunk, lanes), jnp.float32)],
        ),
        out_shape=[out, out],
        cost_estimate=pl.CostEstimate(flops=size * 10, bytes_accessed=size * 9, transcendentals=0),
    )(place, own, from_z, from_y)


def matmul_rows(left, right):
    out = []
    for v in range(len(left)):
        real = imag = None
        for m in range(v + 1):
            a = left[v][0][m : m + 1, :]
            b = left[v][1][m : m + 1, :]
            r, i = right[m]
            term_real, term_imag = a * r - b * i, a * i + b * r
            real = term_real if real is None else real + term_real
            imag = term_imag if imag is None else imag + term_imag
        out.append((real, imag))
    return out


def invert_factor(gram, width, padded):
    row_of = lax.broadcasted_iota(jnp.int32, gram[0][0].shape, 0)
    mean = gram[0][0][0:1, :]
    for v in range(1, width):
        mean = mean + gram[v][0][v : v + 1, :]
    ridge = 0.05 * (mean / width + 1e-06)
    rows = [(jnp.where(row_of == v, r + ridge, r), i) for v, (r, i) in enumerate(gram)]
    zero = jnp.zeros_like(rows[0][0])
    inverse = [(jnp.where(row_of == v, 1.0, zero), zero) for v in range(width)]
    for k in range(width):
        scale = 1.0 / jnp.sqrt(rows[k][0][k : k + 1, :])
        pivot = (rows[k][0] * scale, rows[k][1] * scale)
        known = (inverse[k][0] * scale, inverse[k][1] * scale)
        inverse[k] = known
        for v in range(k + 1, width):
            a = pivot[0][v : v + 1, :]
            b = -pivot[1][v : v + 1, :]
            r, i = rows[v]
            rows[v] = (r - (a * pivot[0] - b * pivot[1]), i - (a * pivot[1] + b * pivot[0]))
            r, i = inverse[v]
            inverse[v] = (r - (a * known[0] - b * known[1]), i - (a * known[1] + b * known[0]))
    return inverse


def factor_kernel(
    vectors, edge, home_ref, row_ref, *refs
):
    sources = refs[: 2 * edge]
    out_ref, tiles, stage, gram, turn, in_sem, out_sem = refs[2 * edge :]
    homes, per_home, _, unit_rows, lanes = tiles.shape
    comps = unit_rows // vectors
    kinds = comps // 2
    count = homes * per_home
    padded = 16
    half = lanes // 2
    norm = 1.0 / (kinds * edge ** 4)
    copies = [
        pltpu.make_async_copy(
            sources[s], tiles.at[home_ref[s], :, row_ref[s]], in_sem.at[s]
        )
        for s in range(2 * edge)
    ]
    for copy in copies:
        copy.start()
    for copy in copies:
        copy.wait()
    zeros = jnp.zeros((padded - vectors, lanes), jnp.float32)
    lane = lax.broadcasted_iota(jnp.int32, (padded, lanes), 1)
    low = lane < half
    sign = jnp.where(low, 1.0, -1.0)

    def operand(n, h):
        home, slot = n // per_home, n % per_home
        plain, turned = [], []
        for k in range(kinds):
            for t in range(edge):
                piece = tiles[home, slot, t, pl.ds(h * kinds + k, vectors, stride=comps), :]
                piece = jnp.concatenate([piece, zeros], axis=0)
                plain.append(piece)
                turned.append(pltpu.roll(piece, half, 1) * sign)
        return jnp.concatenate(
            [jnp.concatenate(plain, axis=1), jnp.concatenate(turned, axis=1)], axis=0
        )

    def gram_of(n, carry):
        for h in range(2):
            both = operand(n, h)
            products = lax.dot_general(
                both[:padded], both, (((1,), (1,)), ((), ())),
                precision=lax.Precision.HIGHEST, preferred_element_type=jnp.float32,
            )
            start = pl.multiple_of((n * 2 + h) * padded, padded)
            gram[pl.ds(start, padded), 0 : 2 * padded] = products * norm
        return carry

    lax.fori_loop(0, count, gram_of, 0)

    batch = gram.shape[0] // padded
    first = []
    for v in range(vectors):
        block = gram[pl.ds(v, batch, stride=padded), :].T
        first.append((block[:padded], block[padded : 2 * padded]))
    inverse = invert_factor(first, vectors, padded)
    moved = matmul_rows(inverse, first)
    for v in range(vectors):
        turn[0, v * padded : (v + 1) * padded, :] = moved[v][0]
        turn[1, v * padded : (v + 1) * padded, :] = moved[v][1]
    for v in range(vectors, padded):
        turn[0, v * padded : (v + 1) * padded, :] = jnp.zeros((padded, batch), jnp.float32)
        turn[1, v * padded : (v + 1) * padded, :] = jnp.zeros((padded, batch), jnp.float32)
    flipped = [
        (turn[0, pl.ds(m, padded, stride=padded), :], -turn[1, pl.ds(m, padded, stride=padded), :])
        for m in range(vectors)
    ]
    second = matmul_rows(inverse, flipped)
    final = matmul_rows(invert_factor(second, vectors, padded), inverse)
    rest = jnp.zeros((lanes - 2 * padded, batch), jnp.float32)
    for w in range(vectors):
        block = jnp.concatenate([final[w][0], final[w][1], rest], axis=0)
        gram[pl.ds(w, batch, stride=padded), :] = block.T

    def out_copy(n, slot):
        return pltpu.make_async_copy(stage.at[slot], out_ref.at[n], out_sem.at[slot])

    def apply_to(n, carry):
        slot = n % 2

        @pl.when(n >= 2)
        def _():
            out_copy(n - 2, slot).wait()

        for h in range(2):
            both = operand(n, h)
            start = pl.multiple_of((n * 2 + h) * padded, padded)
            mixing = gram[pl.ds(start, padded), 0 : 2 * padded]
            made = jnp.dot(
                mixing, both,
                precision=lax.Precision.HIGHEST, preferred_element_type=jnp.float32,
            )
            for k in range(kinds):
                for s in range(edge // 2):
                    at = (k * edge + 2 * s) * lanes
                    one = made[:, at : at + lanes]
                    two = made[:, at + lanes : at + 2 * lanes]
                    real = jnp.where(low, one, pltpu.roll(two, half, 1))
                    imag = jnp.where(low, pltpu.roll(one, half, 1), two)
                    row = k * edge + 2 * s
                    stride = kinds * edge
                    stage[slot, h, pl.ds(row, vectors, stride=stride), :] = real[:vectors]
                    stage[slot, h, pl.ds(row + 1, vectors, stride=stride), :] = imag[:vectors]
        out_copy(n, slot).start()
        return carry

    lax.fori_loop(0, count, apply_to, 0)
    out_copy(count - 2, 0).wait()
    out_copy(count - 1, 1).wait()


def factor(vectors, homes_of, rows_of, homes, buffers):
    edge = len(buffers) // 2
    per_home, unit_rows, lanes = buffers[0].shape
    comps = unit_rows // vectors
    count = homes * per_home
    out_rows = vectors * comps // 2 * edge
    size = count * edge * unit_rows * lanes
    return pl.pallas_call(
        functools.partial(factor_kernel, vectors, edge),
        in_specs=[pl.BlockSpec(memory_space=pltpu.SMEM)] * 2
        + [pl.BlockSpec(memory_space=pl.ANY)] * len(buffers),
        out_specs=pl.BlockSpec(memory_space=pl.ANY),
        out_shape=jax.ShapeDtypeStruct((count, 2, out_rows, lanes), jnp.float32),
        scratch_shapes=[
            pltpu.VMEM((homes, per_home, edge, unit_rows, lanes), jnp.float32),
            pltpu.VMEM((2, 2, out_rows, lanes), jnp.float32),
            pltpu.VMEM((LANES * 16, lanes), jnp.float32),
            pltpu.VMEM((2, 16 * 16, LANES), jnp.float32),
            pltpu.SemaphoreType.DMA((2 * edge,)),
            pltpu.SemaphoreType.DMA((2,)),
        ],
        compiler_params=pltpu.CompilerParams(vmem_limit_bytes=48 * 1024 * 1024),
        cost_estimate=pl.CostEstimate(flops=size * 100, bytes_accessed=size * 8, transcendentals=0),
    )(homes_of, rows_of, *buffers)


def shift_down(array, axis):
    length = lax.axis_size(axis)
    return lax.ppermute(array, axis, [(i, (i - 1) % length) for i in range(length)])


def exchange_rows(oz, oy, place, *rows):
    edge = len(rows)
    from_z = [shift_down(row[:oz], "gz") for row in rows]
    from_y = [
        shift_down(jnp.concatenate([row[oz:, :oy], below[:, :oy]], axis=0), "gy")
        for row, below in zip(rows, from_z)
    ]
    kept, received = [], []
    for t in range(edge):
        keep, send = regroup(oz, oy, place[t], rows[t], from_z[t], from_y[t])
        kept.append(keep)
        received.append(shift_down(send, "ta"))
    return tuple(kept + received)


def per_device_pair(near_null, offsets, owner_slot):
    edge = near_null.shape[0]
    vectors, comps = near_null.shape[3:5]
    me = lax.axis_index("ta").astype(jnp.int32)
    slots = owner_slot.reshape(-1)
    count = slots.shape[0]
    per_home = count // 2
    other_slots = shift_down(slots, "ta")
    t_of = jnp.arange(edge, dtype=jnp.int32)
    stays = t_of >= offsets[0]
    row_slots = jnp.where(stays[:, None], slots[None, :], other_slots[None, :])
    sends = (row_slots // per_home) != me
    place = row_slots % per_home + jnp.where(sends, per_home, 0)
    homes_kept = jnp.where(stays, me, 1 - me)
    homes_of = jnp.concatenate([homes_kept, 1 - homes_kept])
    row_at = jnp.remainder(t_of - offsets[0] + edge, edge)
    rows_of = jnp.concatenate([row_at, row_at])
    x_offset = offsets[3:4]
    rows = [compact(near_null, x_offset, t) for t in range(edge)]
    branches = [
        functools.partial(exchange_rows, oz, oy)
        for oz in range(1, MAX_OFFSET + 1)
        for oy in range(1, MAX_OFFSET + 1)
    ]
    which = (offsets[1] - 1) * MAX_OFFSET + offsets[2] - 1
    buffers = lax.switch(which, branches, place, *rows)
    made = factor(vectors, homes_of, rows_of, 2, buffers)
    kinds = comps // 2
    made = made.reshape(count, 2, vectors, kinds, edge // 2, 2, made.shape[-1])
    return made.transpose(0, 1, 2, 3, 5, 4, 6).reshape(
        count, 2, vectors, kinds, 2, edge // 2 * made.shape[-1]
    )


ridge_scale = 0.05
top_precision = lax.Precision.HIGHEST


def from_behind(array, axis, by):
    length = lax.axis_size(axis)
    return lax.ppermute(array, axis, [(i, (i + by) % length) for i in range(length)])


def factor_pass(blocks):
    norm_count = blocks.shape[3] * blocks.shape[5]
    products = (
        jnp.einsum("nkvcas,nkwcbs->nkavbw", blocks, blocks, precision=top_precision) / norm_count
    )
    gram_real = products[:, :, 0, :, 0, :] + products[:, :, 1, :, 1, :]
    gram_imag = products[:, :, 0, :, 1, :] - products[:, :, 1, :, 0, :]
    width = gram_real.shape[-1]
    diag_mean = jnp.mean(jnp.diagonal(gram_real, axis1=2, axis2=3), axis=-1)
    ridge_term = ridge_scale * (diag_mean + 1e-06)
    gram_real = jnp.moveaxis(gram_real, (2, 3), (0, 1))
    gram_imag = jnp.moveaxis(gram_imag, (2, 3), (0, 1))
    zero_batch = jnp.zeros_like(ridge_term)
    low_real = [[zero_batch] * width for row_idx in range(width)]
    low_imag = [[zero_batch] * width for row_idx in range(width)]
    for col_idx in range(width):
        remain = gram_real[col_idx, col_idx] + ridge_term
        for mid_idx in range(col_idx):
            remain = remain - low_real[col_idx][mid_idx] * low_real[col_idx][mid_idx]
            remain = remain - low_imag[col_idx][mid_idx] * low_imag[col_idx][mid_idx]
        diag_val = jnp.sqrt(remain)
        low_real[col_idx][col_idx] = diag_val
        for row_idx in range(col_idx + 1, width):
            sum_real = gram_real[row_idx, col_idx]
            sum_imag = gram_imag[row_idx, col_idx]
            for mid_idx in range(col_idx):
                left_real = low_real[row_idx][mid_idx]
                left_imag = low_imag[row_idx][mid_idx]
                right_real = low_real[col_idx][mid_idx]
                right_imag = low_imag[col_idx][mid_idx]
                sum_real = sum_real - (left_real * right_real + left_imag * right_imag)
                sum_imag = sum_imag - (left_imag * right_real - left_real * right_imag)
            low_real[row_idx][col_idx] = sum_real / diag_val
            low_imag[row_idx][col_idx] = sum_imag / diag_val
    inv_real = [[zero_batch] * width for row_idx in range(width)]
    inv_imag = [[zero_batch] * width for row_idx in range(width)]
    for col_idx in range(width):
        inv_real[col_idx][col_idx] = 1.0 / low_real[col_idx][col_idx]
        for row_idx in range(col_idx + 1, width):
            sum_real = zero_batch
            sum_imag = zero_batch
            for mid_idx in range(col_idx, row_idx):
                left_real = low_real[row_idx][mid_idx]
                left_imag = low_imag[row_idx][mid_idx]
                right_real = inv_real[mid_idx][col_idx]
                right_imag = inv_imag[mid_idx][col_idx]
                sum_real = sum_real + left_real * right_real - left_imag * right_imag
                sum_imag = sum_imag + left_real * right_imag + left_imag * right_real
            inv_real[row_idx][col_idx] = -sum_real / low_real[row_idx][row_idx]
            inv_imag[row_idx][col_idx] = -sum_imag / low_real[row_idx][row_idx]
    map_real = jnp.stack(
        [
            jnp.stack([inv_real[w_idx][v_idx] for w_idx in range(width)], axis=-1)
            for v_idx in range(width)
        ],
        axis=-2,
    )
    map_imag = -jnp.stack(
        [
            jnp.stack([inv_imag[w_idx][v_idx] for w_idx in range(width)], axis=-1)
            for v_idx in range(width)
        ],
        axis=-2,
    )
    mixing = jnp.stack(
        [jnp.stack([map_real, map_imag], axis=3), jnp.stack([-map_imag, map_real], axis=3)], axis=2
    )
    return jnp.einsum("nkvcas,nkavbw->nkwcbs", blocks, mixing, precision=top_precision)


def two_passes(blocks):
    return factor_pass(factor_pass(blocks))


def arrange(lattice, row_count, agg_edge):
    vector_count = lattice.shape[3]
    comp_count = lattice.shape[4]
    x_sites = lattice.shape[6]
    groups = x_sites // agg_edge
    pieces = lattice.reshape(
        row_count, agg_edge, agg_edge, vector_count, 2, comp_count // 2, 2, groups, agg_edge
    )
    pieces = pieces.transpose(7, 4, 3, 5, 6, 0, 1, 2, 8)
    return pieces.reshape(
        groups, 2, vector_count, comp_count // 2, 2, row_count * agg_edge * agg_edge * agg_edge
    )


def invert(slot_row):
    places = jnp.arange(slot_row.shape[0], dtype=jnp.int32)
    return jnp.sum(jnp.where(slot_row[None, :] == places[:, None], places[None, :], 0), axis=1)


def per_device_general(near_null, offsets, owner_slot):
    agg_edge = near_null.shape[0]
    rim_rows = agg_edge - 1
    from_z = from_behind(near_null[:, :rim_rows], "gz", -1)
    lattice = lax.dynamic_slice_in_dim(
        jnp.concatenate([near_null, from_z], axis=1), offsets[1], agg_edge, 1
    )
    from_y = from_behind(lattice[:, :, :rim_rows], "gy", -1)
    lattice = lax.dynamic_slice_in_dim(
        jnp.concatenate([lattice, from_y], axis=2), offsets[2], agg_edge, 2
    )
    x_sites = lattice.shape[5] // 2
    lattice = lattice.reshape(lattice.shape[:5] + (2, x_sites))
    lattice = lax.dynamic_slice_in_dim(
        jnp.concatenate([lattice, lattice], axis=6), offsets[3], x_sites, 6
    )
    slot_row = owner_slot.reshape(-1)
    source_of = invert(slot_row)
    from_t = from_behind(lattice[:rim_rows], "ta", -1)
    lattice = lax.dynamic_slice_in_dim(
        jnp.concatenate([lattice, from_t], axis=0), offsets[0], agg_edge, 0
    )
    tiles = arrange(lattice, agg_edge, agg_edge)
    packed = jnp.take(tiles, source_of, axis=0)
    result = two_passes(lax.all_to_all(packed, "ta", split_axis=0, concat_axis=0, tiled=True))
    return result


def solution(mesh):
    pair = mesh.shape["ta"] == 2
    return jax.shard_map(
        per_device_pair if pair else per_device_general,
        mesh=mesh,
        in_specs=(P("ta", "gz", "gy", None, None, None), P(), P("ta", "gz", "gy", None)),
        out_specs=P(("ta", "gz", "gy"), None, None, None, None, None),
        check_vma=False,
    )
```

```python
import functools

import jax
import jax.numpy as jnp
from jax import lax
from jax.experimental import pallas as pl
from jax.experimental.pallas import tpu as pltpu
from jax.sharding import PartitionSpec as P

MAX_OFFSET = 3
LANES = 128


def pack_kernel(oz, oy, edge, own_ref, z_ref, out_ref):
    rows = out_ref.shape[2]
    for z in range(edge):
        ref, zi = (z_ref, z + oz - edge) if z + oz >= edge else (own_ref, z + oz)
        for y in range(oy):
            out_ref[z, y] = ref[zi, pl.ds(y, rows, stride=edge), :]


def pack(oz, oy, edge, own, from_z):
    all_rows, lanes = own.shape[1:]
    rows = all_rows // edge
    chunk = rows // 3
    size = edge * oy * rows * lanes
    return pl.pallas_call(
        functools.partial(pack_kernel, oz, oy, edge),
        grid=(rows // chunk,),
        in_specs=[
            pl.BlockSpec((array.shape[0], chunk * edge, lanes), lambda r: (0, r, 0))
            for array in (own, from_z)
        ],
        out_specs=pl.BlockSpec((edge, oy, chunk, lanes), lambda r: (0, 0, r, 0)),
        out_shape=jax.ShapeDtypeStruct((edge, oy, rows, lanes), jnp.float32),
        cost_estimate=pl.CostEstimate(flops=size, bytes_accessed=size * 8, transcendentals=0),
    )(own, from_z)


def regroup_kernel(
    oz, oy, edge, place_ref, shift_ref, own_ref, z_ref, y_ref, keep_ref, send_ref, stage
):
    rows, lanes = y_ref.shape[2:]
    x_sites = lanes // 2
    shift = shift_ref[0]
    count = edge * edge
    half = count // 2
    lane = lax.broadcasted_iota(jnp.int32, (8, lanes), 1)
    places = [place_ref[j] for j in range(count)]
    inside = lane % x_sites < x_sites - shift
    def regroup_rows(step_index, carry):
        r = pl.multiple_of(step_index * 8, 8)
        units = []
        for z in range(edge):
            for y in range(edge):
                if y + oy >= edge:
                    unit = y_ref[z, y + oy - edge, pl.ds(r, 8), :]
                else:
                    ref, zi = (z_ref, z + oz - edge) if z + oz >= edge else (own_ref, z + oz)
                    unit = ref[zi, pl.ds(r * edge + y + oy, 8, stride=edge), :]
                near = pltpu.roll(unit, lanes - shift, 1)
                wrap = pltpu.roll(unit, x_sites - shift, 1)
                units.append(jnp.where(inside, near, wrap))
        bit = 1
        while bit < count:
            step = bit * edge
            high = (lane & step) != 0
            fresh = list(units)
            for u in range(count):
                if not u & bit:
                    low_unit, high_unit = units[u], units[u + bit]
                    fresh[u] = jnp.where(high, pltpu.roll(high_unit, step, 1), low_unit)
                    fresh[u + bit] = jnp.where(
                        high, high_unit, pltpu.roll(low_unit, lanes - step, 1)
                    )
            units = fresh
            bit *= 2
        for j in range(count):
            stage[places[j], pl.ds(r, 8), :] = units[j]
        return carry

    lax.fori_loop(0, rows // 8, regroup_rows, 0)
    keep_ref[...] = stage[:half]
    send_ref[...] = stage[half:]


def regroup(oz, oy, place, x_offset, own, from_z, from_y):
    edge = own.shape[0]
    rows, lanes = from_y.shape[2:]
    chunk = rows // 3
    count = edge * edge
    half = count // 2
    size = count * rows * lanes
    out = jax.ShapeDtypeStruct((half, rows, lanes), jnp.float32)
    out_spec = pl.BlockSpec((half, chunk, lanes), lambda r, s, x: (0, r, 0))
    return pl.pallas_call(
        functools.partial(regroup_kernel, oz, oy, edge),
        grid_spec=pltpu.PrefetchScalarGridSpec(
            num_scalar_prefetch=2,
            grid=(rows // chunk,),
            in_specs=[
                pl.BlockSpec((array.shape[0], chunk * edge, lanes), lambda r, s, x: (0, r, 0))
                for array in (own, from_z)
            ]
            + [pl.BlockSpec(from_y.shape[:2] + (chunk, lanes), lambda r, s, x: (0, 0, r, 0))],
            out_specs=[out_spec, out_spec],
            scratch_shapes=[pltpu.VMEM((count, chunk, lanes), jnp.float32)],
        ),
        out_shape=[out, out],
        cost_estimate=pl.CostEstimate(flops=size * 10, bytes_accessed=size * 9, transcendentals=0),
    )(place, x_offset, own, from_z, from_y)


def matmul_rows(left, right):
    out = []
    for v in range(len(left)):
        real = imag = None
        for m in range(v + 1):
            a = left[v][0][m : m + 1, :]
            b = left[v][1][m : m + 1, :]
            r, i = right[m]
            term_real, term_imag = a * r - b * i, a * i + b * r
            real = term_real if real is None else real + term_real
            imag = term_imag if imag is None else imag + term_imag
        out.append((real, imag))
    return out


def invert_factor(gram, width, padded):
    row_of = lax.broadcasted_iota(jnp.int32, gram[0][0].shape, 0)
    mean = gram[0][0][0:1, :]
    for v in range(1, width):
        mean = mean + gram[v][0][v : v + 1, :]
    ridge = 0.05 * (mean / width + 1e-06)
    rows = [(jnp.where(row_of == v, r + ridge, r), i) for v, (r, i) in enumerate(gram)]
    zero = jnp.zeros_like(rows[0][0])
    inverse = [(jnp.where(row_of == v, 1.0, zero), zero) for v in range(width)]
    for k in range(width):
        scale = 1.0 / jnp.sqrt(rows[k][0][k : k + 1, :])
        pivot = (rows[k][0] * scale, rows[k][1] * scale)
        known = (inverse[k][0] * scale, inverse[k][1] * scale)
        inverse[k] = known
        for v in range(k + 1, width):
            a = pivot[0][v : v + 1, :]
            b = -pivot[1][v : v + 1, :]
            r, i = rows[v]
            rows[v] = (r - (a * pivot[0] - b * pivot[1]), i - (a * pivot[1] + b * pivot[0]))
            r, i = inverse[v]
            inverse[v] = (r - (a * known[0] - b * known[1]), i - (a * known[1] + b * known[0]))
    return inverse


def factor_kernel(
    vectors, edge, home_ref, row_ref, *refs
):
    sources = refs[: 2 * edge]
    out_ref, tiles, stage, gram, turn, in_sem, out_sem = refs[2 * edge :]
    homes, per_home, _, unit_rows, lanes = tiles.shape
    comps = unit_rows // vectors
    kinds = comps // 2
    count = homes * per_home
    padded = 16
    half = lanes // 2
    norm = 1.0 / (kinds * edge ** 4)
    copies = [
        pltpu.make_async_copy(
            sources[s], tiles.at[home_ref[s], :, row_ref[s]], in_sem.at[s]
        )
        for s in range(2 * edge)
    ]
    for copy in copies:
        copy.start()
    for copy in copies:
        copy.wait()
    zeros = jnp.zeros((padded - vectors, lanes), jnp.float32)
    lane = lax.broadcasted_iota(jnp.int32, (padded, lanes), 1)
    low = lane < half
    sign = jnp.where(low, 1.0, -1.0)

    def operand(n, h):
        home, slot = n // per_home, n % per_home
        plain, turned = [], []
        for k in range(kinds):
            for t in range(edge):
                piece = tiles[home, slot, t, pl.ds(h * kinds + k, vectors, stride=comps), :]
                piece = jnp.concatenate([piece, zeros], axis=0)
                plain.append(piece)
                turned.append(pltpu.roll(piece, half, 1) * sign)
        return jnp.concatenate(
            [jnp.concatenate(plain, axis=1), jnp.concatenate(turned, axis=1)], axis=0
        )

    def gram_of(n, carry):
        for h in range(2):
            both = operand(n, h)
            products = lax.dot_general(
                both[:padded], both, (((1,), (1,)), ((), ())),
                precision=lax.Precision.HIGHEST, preferred_element_type=jnp.float32,
            )
            start = pl.multiple_of((n * 2 + h) * padded, padded)
            gram[pl.ds(start, padded), 0 : 2 * padded] = products * norm
        return carry

    lax.fori_loop(0, count, gram_of, 0)

    batch = gram.shape[0] // padded
    first = []
    for v in range(vectors):
        block = gram[pl.ds(v, batch, stride=padded), :].T
        first.append((block[:padded], block[padded : 2 * padded]))
    inverse = invert_factor(first, vectors, padded)
    moved = matmul_rows(inverse, first)
    for v in range(vectors):
        turn[0, v * padded : (v + 1) * padded, :] = moved[v][0]
        turn[1, v * padded : (v + 1) * padded, :] = moved[v][1]
    for v in range(vectors, padded):
        turn[0, v * padded : (v + 1) * padded, :] = jnp.zeros((padded, batch), jnp.float32)
        turn[1, v * padded : (v + 1) * padded, :] = jnp.zeros((padded, batch), jnp.float32)
    flipped = [
        (turn[0, pl.ds(m, padded, stride=padded), :], -turn[1, pl.ds(m, padded, stride=padded), :])
        for m in range(vectors)
    ]
    second = matmul_rows(inverse, flipped)
    final = matmul_rows(invert_factor(second, vectors, padded), inverse)
    rest = jnp.zeros((lanes - 2 * padded, batch), jnp.float32)
    for w in range(vectors):
        block = jnp.concatenate([final[w][0], final[w][1], rest], axis=0)
        gram[pl.ds(w, batch, stride=padded), :] = block.T

    def out_copy(n, slot):
        return pltpu.make_async_copy(stage.at[slot], out_ref.at[n], out_sem.at[slot])

    def apply_to(n, carry):
        slot = n % 2

        @pl.when(n >= 2)
        def _():
            out_copy(n - 2, slot).wait()

        for h in range(2):
            both = operand(n, h)
            start = pl.multiple_of((n * 2 + h) * padded, padded)
            mixing = gram[pl.ds(start, padded), 0 : 2 * padded]
            made = jnp.dot(
                mixing, both,
                precision=lax.Precision.HIGHEST, preferred_element_type=jnp.float32,
            )
            for k in range(kinds):
                for s in range(edge // 2):
                    at = (k * edge + 2 * s) * lanes
                    one = made[:, at : at + lanes]
                    two = made[:, at + lanes : at + 2 * lanes]
                    real = jnp.where(low, one, pltpu.roll(two, half, 1))
                    imag = jnp.where(low, pltpu.roll(one, half, 1), two)
                    row = k * edge + 2 * s
                    stride = kinds * edge
                    stage[slot, h, pl.ds(row, vectors, stride=stride), :] = real[:vectors]
                    stage[slot, h, pl.ds(row + 1, vectors, stride=stride), :] = imag[:vectors]
        out_copy(n, slot).start()
        return carry

    lax.fori_loop(0, count, apply_to, 0)
    out_copy(count - 2, 0).wait()
    out_copy(count - 1, 1).wait()


def factor(vectors, homes_of, rows_of, homes, buffers):
    edge = len(buffers) // 2
    per_home, unit_rows, lanes = buffers[0].shape
    comps = unit_rows // vectors
    count = homes * per_home
    out_rows = vectors * comps // 2 * edge
    size = count * edge * unit_rows * lanes
    return pl.pallas_call(
        functools.partial(factor_kernel, vectors, edge),
        in_specs=[pl.BlockSpec(memory_space=pltpu.SMEM)] * 2
        + [pl.BlockSpec(memory_space=pl.ANY)] * len(buffers),
        out_specs=pl.BlockSpec(memory_space=pl.ANY),
        out_shape=jax.ShapeDtypeStruct((count, 2, out_rows, lanes), jnp.float32),
        scratch_shapes=[
            pltpu.VMEM((homes, per_home, edge, unit_rows, lanes), jnp.float32),
            pltpu.VMEM((2, 2, out_rows, lanes), jnp.float32),
            pltpu.VMEM((LANES * 16, lanes), jnp.float32),
            pltpu.VMEM((2, 16 * 16, LANES), jnp.float32),
            pltpu.SemaphoreType.DMA((2 * edge,)),
            pltpu.SemaphoreType.DMA((2,)),
        ],
        compiler_params=pltpu.CompilerParams(vmem_limit_bytes=48 * 1024 * 1024),
        cost_estimate=pl.CostEstimate(flops=size * 100, bytes_accessed=size * 8, transcendentals=0),
    )(homes_of, rows_of, *buffers)


def shift_down(array, axis):
    length = lax.axis_size(axis)
    return lax.ppermute(array, axis, [(i, (i - 1) % length) for i in range(length)])


def exchange_rows(oz, oy, offsets, slots, lattice):
    edge = lattice.shape[0]
    rows = [lattice[t] for t in range(edge)]
    from_z = [shift_down(row[:oz], "gz") for row in rows]
    me = lax.axis_index("ta").astype(jnp.int32)
    per_home = slots.shape[0] // 2
    other_slots = shift_down(slots, "ta")
    stays = jnp.arange(edge, dtype=jnp.int32) >= offsets[0]
    row_slots = jnp.where(stays[:, None], slots[None, :], other_slots[None, :])
    sends = (row_slots // per_home) != me
    place = row_slots % per_home + jnp.where(sends, per_home, 0)
    from_y = [
        shift_down(pack(oz, oy, edge, row, below), "gy") for row, below in zip(rows, from_z)
    ]
    kept, received = [], []
    for t in range(edge):
        keep, send = regroup(oz, oy, place[t], offsets[3:4], rows[t], from_z[t], from_y[t])
        kept.append(keep)
        received.append(shift_down(send, "ta"))
    return tuple(kept + received)


def per_device_pair(near_null, offsets, owner_slot):
    edge = near_null.shape[0]
    vectors, comps = near_null.shape[3:5]
    me = lax.axis_index("ta").astype(jnp.int32)
    slots = owner_slot.reshape(-1)
    count = slots.shape[0]
    t_of = jnp.arange(edge, dtype=jnp.int32)
    stays = t_of >= offsets[0]
    homes_kept = jnp.where(stays, me, 1 - me)
    homes_of = jnp.concatenate([homes_kept, 1 - homes_kept])
    row_at = jnp.remainder(t_of - offsets[0] + edge, edge)
    rows_of = jnp.concatenate([row_at, row_at])
    lattice = near_null.transpose(0, 1, 3, 4, 2, 5).reshape(
        edge, near_null.shape[1], -1, near_null.shape[5]
    )
    branches = [
        functools.partial(exchange_rows, oz, oy)
        for oz in range(1, MAX_OFFSET + 1)
        for oy in range(1, MAX_OFFSET + 1)
    ]
    which = (offsets[1] - 1) * MAX_OFFSET + offsets[2] - 1
    buffers = lax.switch(which, branches, offsets, slots, lattice)
    made = factor(vectors, homes_of, rows_of, 2, buffers)
    kinds = comps // 2
    made = made.reshape(count, 2, vectors, kinds, edge // 2, 2, made.shape[-1])
    return made.transpose(0, 1, 2, 3, 5, 4, 6).reshape(
        count, 2, vectors, kinds, 2, edge // 2 * made.shape[-1]
    )


ridge_scale = 0.05
top_precision = lax.Precision.HIGHEST


def from_behind(array, axis, by):
    length = lax.axis_size(axis)
    return lax.ppermute(array, axis, [(i, (i + by) % length) for i in range(length)])


def factor_pass(blocks):
    norm_count = blocks.shape[3] * blocks.shape[5]
    products = (
        jnp.einsum("nkvcas,nkwcbs->nkavbw", blocks, blocks, precision=top_precision) / norm_count
    )
    gram_real = products[:, :, 0, :, 0, :] + products[:, :, 1, :, 1, :]
    gram_imag = products[:, :, 0, :, 1, :] - products[:, :, 1, :, 0, :]
    width = gram_real.shape[-1]
    diag_mean = jnp.mean(jnp.diagonal(gram_real, axis1=2, axis2=3), axis=-1)
    ridge_term = ridge_scale * (diag_mean + 1e-06)
    gram_real = jnp.moveaxis(gram_real, (2, 3), (0, 1))
    gram_imag = jnp.moveaxis(gram_imag, (2, 3), (0, 1))
    zero_batch = jnp.zeros_like(ridge_term)
    low_real = [[zero_batch] * width for row_idx in range(width)]
    low_imag = [[zero_batch] * width for row_idx in range(width)]
    for col_idx in range(width):
        remain = gram_real[col_idx, col_idx] + ridge_term
        for mid_idx in range(col_idx):
            remain = remain - low_real[col_idx][mid_idx] * low_real[col_idx][mid_idx]
            remain = remain - low_imag[col_idx][mid_idx] * low_imag[col_idx][mid_idx]
        diag_val = jnp.sqrt(remain)
        low_real[col_idx][col_idx] = diag_val
        for row_idx in range(col_idx + 1, width):
            sum_real = gram_real[row_idx, col_idx]
            sum_imag = gram_imag[row_idx, col_idx]
            for mid_idx in range(col_idx):
                left_real = low_real[row_idx][mid_idx]
                left_imag = low_imag[row_idx][mid_idx]
                right_real = low_real[col_idx][mid_idx]
                right_imag = low_imag[col_idx][mid_idx]
                sum_real = sum_real - (left_real * right_real + left_imag * right_imag)
                sum_imag = sum_imag - (left_imag * right_real - left_real * right_imag)
            low_real[row_idx][col_idx] = sum_real / diag_val
            low_imag[row_idx][col_idx] = sum_imag / diag_val
    inv_real = [[zero_batch] * width for row_idx in range(width)]
    inv_imag = [[zero_batch] * width for row_idx in range(width)]
    for col_idx in range(width):
        inv_real[col_idx][col_idx] = 1.0 / low_real[col_idx][col_idx]
        for row_idx in range(col_idx + 1, width):
            sum_real = zero_batch
            sum_imag = zero_batch
            for mid_idx in range(col_idx, row_idx):
                left_real = low_real[row_idx][mid_idx]
                left_imag = low_imag[row_idx][mid_idx]
                right_real = inv_real[mid_idx][col_idx]
                right_imag = inv_imag[mid_idx][col_idx]
                sum_real = sum_real + left_real * right_real - left_imag * right_imag
                sum_imag = sum_imag + left_real * right_imag + left_imag * right_real
            inv_real[row_idx][col_idx] = -sum_real / low_real[row_idx][row_idx]
            inv_imag[row_idx][col_idx] = -sum_imag / low_real[row_idx][row_idx]
    map_real = jnp.stack(
        [
            jnp.stack([inv_real[w_idx][v_idx] for w_idx in range(width)], axis=-1)
            for v_idx in range(width)
        ],
        axis=-2,
    )
    map_imag = -jnp.stack(
        [
            jnp.stack([inv_imag[w_idx][v_idx] for w_idx in range(width)], axis=-1)
            for v_idx in range(width)
        ],
        axis=-2,
    )
    mixing = jnp.stack(
        [jnp.stack([map_real, map_imag], axis=3), jnp.stack([-map_imag, map_real], axis=3)], axis=2
    )
    return jnp.einsum("nkvcas,nkavbw->nkwcbs", blocks, mixing, precision=top_precision)


def two_passes(blocks):
    return factor_pass(factor_pass(blocks))


def arrange(lattice, row_count, agg_edge):
    vector_count = lattice.shape[3]
    comp_count = lattice.shape[4]
    x_sites = lattice.shape[6]
    groups = x_sites // agg_edge
    pieces = lattice.reshape(
        row_count, agg_edge, agg_edge, vector_count, 2, comp_count // 2, 2, groups, agg_edge
    )
    pieces = pieces.transpose(7, 4, 3, 5, 6, 0, 1, 2, 8)
    return pieces.reshape(
        groups, 2, vector_count, comp_count // 2, 2, row_count * agg_edge * agg_edge * agg_edge
    )


def invert(slot_row):
    places = jnp.arange(slot_row.shape[0], dtype=jnp.int32)
    return jnp.sum(jnp.where(slot_row[None, :] == places[:, None], places[None, :], 0), axis=1)


def per_device_general(near_null, offsets, owner_slot):
    agg_edge = near_null.shape[0]
    rim_rows = agg_edge - 1
    from_z = from_behind(near_null[:, :rim_rows], "gz", -1)
    lattice = lax.dynamic_slice_in_dim(
        jnp.concatenate([near_null, from_z], axis=1), offsets[1], agg_edge, 1
    )
    from_y = from_behind(lattice[:, :, :rim_rows], "gy", -1)
    lattice = lax.dynamic_slice_in_dim(
        jnp.concatenate([lattice, from_y], axis=2), offsets[2], agg_edge, 2
    )
    x_sites = lattice.shape[5] // 2
    lattice = lattice.reshape(lattice.shape[:5] + (2, x_sites))
    lattice = lax.dynamic_slice_in_dim(
        jnp.concatenate([lattice, lattice], axis=6), offsets[3], x_sites, 6
    )
    slot_row = owner_slot.reshape(-1)
    source_of = invert(slot_row)
    from_t = from_behind(lattice[:rim_rows], "ta", -1)
    lattice = lax.dynamic_slice_in_dim(
        jnp.concatenate([lattice, from_t], axis=0), offsets[0], agg_edge, 0
    )
    tiles = arrange(lattice, agg_edge, agg_edge)
    packed = jnp.take(tiles, source_of, axis=0)
    result = two_passes(lax.all_to_all(packed, "ta", split_axis=0, concat_axis=0, tiled=True))
    return result


def solution(mesh):
    pair = mesh.shape["ta"] == 2
    return jax.shard_map(
        per_device_pair if pair else per_device_general,
        mesh=mesh,
        in_specs=(P("ta", "gz", "gy", None, None, None), P(), P("ta", "gz", "gy", None)),
        out_specs=P(("ta", "gz", "gy"), None, None, None, None, None),
        check_vma=False,
    )
```
